256 devices in a mesh: dp: 16 (over z_hi, y), ctx: 4 (over x), head: 4 (over z_lo, core).
Axes of the slice: x: 4, y: 4, z: 8 (z_hi: 4, z_lo: 2; z = z_hi * 2 + z_lo), core: 2. Of those that a mesh axis runs over, the one named last changes fastest.
Arguments:
- mix_query: bfloat16 [32768, 8192], P(('dp', 'ctx', 'head')), parts along dimension 0, may hold values from -6 to 6
- mix_key: bfloat16 [32768, 8192], P(('dp', 'ctx', 'head')), parts along dimension 0, may hold values from -6 to 6
- mix_value: bfloat16 [32768, 8192], P(('dp', 'ctx', 'head')), parts along dimension 0, may hold values from -6 to 6
- mr_filter: bfloat16 [512, 128], replicated, may hold values from -0.5 to 0.5
- doc_ids: int32 [32768], P('dp'), parts along dimension 0, may hold values from 0 to 3, never falling along the last dimension, each value on 1 to 1536 neighbouring positions
- att_query: bfloat16 [32768, 4096], P(('dp', 'ctx'), 'head'), parts along dimension 0, may hold values from -5 to 5
- att_key: bfloat16 [32768, 4096], P(('dp', 'ctx'), 'head'), parts along dimension 0, may hold values from -5 to 5
- att_value: bfloat16 [32768, 4096], P(('dp', 'ctx'), 'head'), parts along dimension 0, may hold values from -6 to 6
Outputs:
- mixed: bfloat16 [32768, 8192], P(('dp', 'ctx', 'head')), parts along dimension 0
- attended: bfloat16 [32768, 4096], P(('dp', 'ctx'), 'head'), parts along dimension 0
The draws below stay inside these ranges and needn't reach their ends.
There are 16 independent parts, one for each index of `dp`. The reference program is written for one: setup_inputs(seed, part) draws one part's arguments, and reference() takes and returns one part's arrays. A program takes and returns all parts, laid end to end along the dimension named above; an argument that names none is the same for every part. Nothing has to cross between parts.
Inputs may be any that keep to these rules, and one draw needn't show every extreme that they name: `doc_ids`: document numbers never fall along the sequence; every number occurs; each document covers 1 to 1536 tokens and one covers exactly 1536.
All inputs are finite; a program needn't handle non-finite values.
Results may differ from the reference program's by a relative error of at most 0.0049.
Values may be sent and summed in bfloat16 or wider, within the bound.
No kernel may reach another device: no remote copies, remote signals or barrier semaphores. Data moves between devices by JAX's collectives and lax.ppermute only.
A program may use at most 128 MiB of HBM per device.

```python
import math
import jax
import jax.numpy as jnp
import numpy as np
from jax import lax

D = 8192
GROUPS = 512
FILT = 128
HEADS = 32
HEAD_DIM = 128
DOCS = 4
SEQ = 2048
LONGEST = 1536


def base_draw(key, salt_value):
    row_width = HEADS * HEAD_DIM
    return jnp.clip(jax.random.normal(jax.random.fold_in(key, salt_value), (SEQ, row_width), jnp.float32), -5.0, 5.0)


def draw_att_query(key, part):
    values_out = base_draw(key, 1)
    return values_out.astype(jnp.bfloat16)


def draw_att_key(key, part):
    values_out = base_draw(key, 2)
    return values_out.astype(jnp.bfloat16)


def level_of(stream_key, shape, split, least, top_value):
    def one(position, blocks):
        heights = jax.random.uniform(jax.random.fold_in(jax.random.fold_in(stream_key, 6), position), (blocks,), jnp.float32, least / len(split), top_value / len(split))
        return jnp.repeat(jnp.exp(heights), shape[position] // blocks).reshape((-1,) + (1,) * (len(shape) - position - 1))

    level = one(*split[0])
    for cut in split[1:]:
        level = level * one(*cut)
    return level


def profile(number_of, total, limit, skew):
    weights = [(1 << 20) // math.isqrt(grade ** skew) + 1 for grade in range(2, number_of + 1)]
    rest, holding = total - limit - (number_of - 1), [1] * (number_of - 1)
    while rest > 0:
        free = [i for i in range(number_of - 1) if holding[i] < limit]
        pool, budget = sum([weights[i] for i in free]), rest
        for i in free:
            extra = min(limit - holding[i], max(1, budget * weights[i] // pool), rest)
            holding[i] = holding[i] + extra
            rest = rest - extra
    return np.array([limit] + holding)


def uneven(rng, number_of, total, most, slope):
    if number_of == 2:
        one = jax.random.randint(rng, (), max(1, total - most), min(most, total - 1) + 1)
        return jnp.stack([one, total - one])
    tallies = jnp.asarray(profile(number_of, total, most, slope), jnp.int32)
    couples = (number_of - 1) // 2
    source_of, receiver = tallies[1:1 + 2 * couples:2], tallies[2:2 + 2 * couples:2]
    margin = jnp.minimum(source_of - 1, most - receiver)
    shifted = jax.random.randint(jax.random.fold_in(rng, 1), (couples,), 0, 1 << 20) % (margin + 1)
    tallies = tallies.at[1:1 + 2 * couples:2].set(source_of - shifted).at[2:2 + 2 * couples:2].set(receiver + shifted)
    return tallies[jax.random.permutation(jax.random.fold_in(rng, 2), number_of)]


def normal_values(key, shape, spread, limit, shards=(), kind=jnp.bfloat16):
    result = spread * jax.random.normal(key, shape, jnp.float32)
    if shards:
        result = result * level_of(key, shape, shards, -0.22, 0.18)
    return jnp.clip(result, -limit, limit).astype(kind)


def setup_inputs(seed: int = 0, part: int = 0) -> dict:
    seeds = jax.random.split(jax.random.key(seed), 9)
    part_splits = jax.random.split(jax.random.fold_in(seeds[8], part), 9)
    mix_query = normal_values(part_splits[0], (SEQ, D), 1.0, 6.0, ((0, 16),))
    mix_key = normal_values(part_splits[1], (SEQ, D), 1.0, 6.0, ((0, 16),))
    mix_value = normal_values(part_splits[2], (SEQ, D), 1.0, 6.0, ((0, 16),))
    mr_filter = normal_values(seeds[3], (GROUPS, FILT), FILT ** -0.5, 0.5)
    doc_ids = jnp.searchsorted(jnp.cumsum(uneven(part_splits[4], DOCS, SEQ, LONGEST, 0)), jnp.arange(SEQ), side="right").astype(jnp.int32)
    att_query = draw_att_query(jax.random.fold_in(jax.random.fold_in(seeds[8], part), 71), part)
    att_key = draw_att_key(jax.random.fold_in(jax.random.fold_in(seeds[8], part), 71), part)
    att_value = normal_values(part_splits[7], (SEQ, HEADS * HEAD_DIM), 1.0, 6.0, ((0, 4), (1, 4)))
    return {"mix_query": mix_query, "mix_key": mix_key, "mix_value": mix_value, "mr_filter": mr_filter, "doc_ids": doc_ids, "att_query": att_query, "att_key": att_key, "att_value": att_value}


NEG_FILL = -1e+30

def toeplitz_rows(filters):
    groups = filters.shape[0]
    filt_len = filters.shape[1]
    lag_index = jnp.arange(filt_len, dtype=jnp.int32)[:, None, None]
    out_index = jnp.arange(filt_len, dtype=jnp.int32)[None, :, None]
    src_index = jnp.arange(2 * filt_len, dtype=jnp.int32)[None, None, :]
    table = (out_index + filt_len - src_index == lag_index).astype(filters.dtype)
    table = table.reshape(filt_len, 2 * filt_len * filt_len)
    kernel = jnp.dot(filters, table, preferred_element_type=jnp.float32).astype(filters.dtype)
    return kernel.reshape(groups, filt_len, 2 * filt_len)

def grouped_conv(extended, seg_ext, filters):
    groups = filters.shape[0]
    filt_len = filters.shape[1]
    channels = extended.shape[1]
    group_size = channels // groups
    blocks = extended.shape[0] // filt_len - 1
    tiled_rows = extended.reshape(blocks + 1, filt_len, groups, group_size)
    paired = jnp.concatenate([tiled_rows[:-1], tiled_rows[1:]], axis=1)
    seg_tiles = seg_ext.reshape(blocks + 1, filt_len)
    seg_pairs = jnp.concatenate([seg_tiles[:-1], seg_tiles[1:]], axis=1)
    same_doc = seg_tiles[1:][:, :, None] == seg_pairs[:, None, :]
    group_step = math.gcd(groups, 64)
    group_blocks = groups // group_step
    pairs_split = jnp.moveaxis(paired.reshape(blocks, 2 * filt_len, group_blocks, group_step, group_size), 2, 0)
    filt_split = filters.reshape(group_blocks, group_step, filt_len)

    def per_groups(operands):
        part_filters, part_pairs = operands
        kernel = toeplitz_rows(part_filters).astype(jnp.float32)
        masked = jnp.where(same_doc[:, None], kernel[None], jnp.zeros((), jnp.float32))
        return jnp.einsum('bgts,bsgc->btgc', masked, part_pairs.astype(jnp.float32), precision=lax.Precision.HIGHEST)
    results = lax.map(per_groups, (filt_split, pairs_split))
    return jnp.moveaxis(results, 0, 2).reshape(blocks * filt_len, channels)

def reference(mix_query, mix_key, mix_value, mr_filter, doc_ids, att_query, att_key, att_value):
    product = (mix_key.astype(jnp.float32) * mix_value.astype(jnp.float32)).astype(jnp.bfloat16)
    filt_len = mr_filter.shape[1]
    extended = jnp.concatenate([jnp.zeros((filt_len, D), jnp.bfloat16), product], axis=0)
    seg_ext = jnp.concatenate([jnp.full((filt_len,), -1, jnp.int32), doc_ids.astype(jnp.int32)])
    convolved = grouped_conv(extended, seg_ext, mr_filter)
    mixed = (mix_query.astype(jnp.float32) * convolved).astype(jnp.bfloat16)
    head_count = att_query.shape[1] // HEAD_DIM
    score_scale = 1.0 / math.sqrt(HEAD_DIM)

    def split_heads(array):
        return jnp.moveaxis(array.reshape(SEQ, head_count, HEAD_DIM), 1, 0)
    positions = jnp.arange(SEQ, dtype=jnp.int32)
    allowed = (positions[None, :] <= positions[:, None]) & (doc_ids[None, :] == doc_ids[:, None])

    def per_head(operands):
        query_head, key_head, value_head = operands
        scores = jnp.dot(query_head, key_head.T, preferred_element_type=jnp.float32) * score_scale
        masked = jnp.where(allowed, scores, NEG_FILL)
        row_max = lax.optimization_barrier(jnp.max(masked, axis=1, keepdims=True))
        weights = jnp.where(allowed, jnp.exp(masked - row_max), 0.0)
        denominator = lax.optimization_barrier(jnp.sum(weights, axis=1, keepdims=True))
        summed = jnp.dot(weights.astype(jnp.bfloat16), value_head, preferred_element_type=jnp.float32)
        return (summed / denominator).astype(jnp.bfloat16)
    outputs = lax.map(per_head, (split_heads(att_query), split_heads(att_key), split_heads(att_value)))
    attended = jnp.moveaxis(outputs, 0, 1).reshape(SEQ, head_count * HEAD_DIM)
    return (mixed, attended)
```

```python
import functools
import math

import jax
import jax.numpy as jnp
from jax import lax
from jax.experimental import pallas as pl
from jax.experimental.pallas import tpu as pltpu
from jax.sharding import PartitionSpec as P

HEAD_DIM = 128
NEG_FILL = -1e30
LOG2_SCALE = math.log2(math.e) / math.sqrt(HEAD_DIM)
SIDE = 4
SUB = 256
EXTRA = 16
COLS = 1024
HEADS_AXIS = 4


def pick(at, *values):
    out = jnp.int32(values[-1])
    for i in range(len(values) - 2, -1, -1):
        out = jnp.where(at == i, jnp.int32(values[i]), out)
    return out


def first_of(bounds, position):
    first = jnp.zeros_like(position)
    for doc in range(1, 4):
        first = jnp.where(bounds[doc] <= position, bounds[doc], first)
    return first


def conv_kernel(group_size, place, bounds, rim_a_ref, rim_b_ref, prod_ref, query_ref, filt_ref, out_ref, mask):
    rows, cols = prod_ref.shape
    step = pl.program_id(0)

    @pl.when(step == 0)
    def _():
        token = place[0] * rows + lax.broadcasted_iota(jnp.int32, (2 * rows, rows), 1)
        source = (place[0] - 1) * rows + lax.broadcasted_iota(jnp.int32, (2 * rows, rows), 0)
        allowed = (source <= token) & (source > token - rows) & (source >= first_of(bounds, token))
        mask[...] = jnp.where(allowed, 1.0, 0.0).astype(jnp.bfloat16)

    rim = jnp.where(step < pl.num_programs(0) // 2, rim_a_ref[...], rim_b_ref[...])
    turned = jnp.concatenate([rim, prod_ref[...]], axis=0).T
    filters = filt_ref[...].astype(jnp.float32)
    allowed = mask[...]
    parts = []
    for g in range(cols // group_size):
        line = jnp.broadcast_to(filters[g : g + 1, :], (rows, rows))
        ring = pltpu.roll(line, 0, 1, stride=1, stride_axis=0).astype(jnp.bfloat16)
        taps = jnp.concatenate([ring, ring], axis=0) * allowed
        parts.append(
            jnp.dot(turned[g * group_size : (g + 1) * group_size], taps, preferred_element_type=jnp.float32)
        )
    total = jnp.concatenate(parts, axis=0).T
    out_ref[...] = (query_ref[...].astype(jnp.float32) * total).astype(out_ref.dtype)


def mixer(place, bounds, rim_a, rim_b, product, mix_query, mr_filter):
    rows, width = product.shape
    groups, filt_len = mr_filter.shape
    group_size = width // groups
    steps = width // COLS
    tile = pl.BlockSpec((rows, COLS), lambda i, *_: (0, i))
    return pl.pallas_call(
        functools.partial(conv_kernel, group_size),
        out_shape=jax.ShapeDtypeStruct((rows, width), jnp.bfloat16),
        grid_spec=pltpu.PrefetchScalarGridSpec(
            num_scalar_prefetch=2,
            grid=(steps,),
            in_specs=[
                pl.BlockSpec((rows, COLS), lambda i, *_: (0, jnp.minimum(i, steps // 2 - 1))),
                pl.BlockSpec((rows, COLS), lambda i, *_: (0, jnp.maximum(i - steps // 2, 0))),
                tile,
                tile,
                pl.BlockSpec((COLS // group_size, filt_len), lambda i, *_: (i, 0)),
            ],
            out_specs=tile,
            scratch_shapes=[pltpu.VMEM((2 * rows, rows), jnp.bfloat16)],
        ),
        cost_estimate=pl.CostEstimate(
            flops=2 * rows * 2 * filt_len * width * 16, bytes_accessed=8 * rows * width, transcendentals=0
        ),
        name="mixer",
    )(place, bounds, rim_a, rim_b, product, mix_query, mr_filter)


def cols_of(h):
    return slice(h * HEAD_DIM, (h + 1) * HEAD_DIM)


def fold_tiles(bounds, query_block, query, sources, heads, state, finish):
    top, den, acc, turned_q, turned_v = state
    rows = query.shape[0]
    turned_q[...] = query.T
    whole_lowest = first_of(bounds, query_block * rows)
    for n, (block, _, value_of) in enumerate(sources):

        @pl.when((block >= 0) & (block <= query_block) & ((block + 1) * rows > whole_lowest))
        def _(n=n, value_of=value_of):
            turned_v[n] = value_of().T

    for part in range(rows // SUB):
        at = pl.ds(part * SUB, SUB)
        query_from = query_block * rows + part * SUB
        line_pos = query_from + lax.broadcasted_iota(jnp.int32, (1, SUB), 1)
        first_row = first_of(bounds, line_pos)
        lowest = first_of(bounds, query_from)
        top[...] = jnp.full(top.shape, 0.5 * NEG_FILL, jnp.float32)
        den[...] = jnp.zeros(den.shape, jnp.float32)
        acc[...] = jnp.zeros(acc.shape, jnp.float32)
        for n, (block, key_of, _) in enumerate(sources):
            for piece in range(rows // SUB):
                key_from = block * rows + piece * SUB
                needed = (block >= 0) & (key_from <= query_from) & (key_from + SUB > lowest)

                @pl.when(needed)
                def _(n=n, key_of=key_of, piece=piece, key_from=key_from):
                    take = pl.ds(piece * SUB, SUB)
                    key_pos = key_from + lax.broadcasted_iota(jnp.int32, (SUB, SUB), 0)
                    allowed = (key_pos <= line_pos) & (key_pos >= first_row)
                    scores = [
                        jnp.dot(key_of(h, take), turned_q[cols_of(h), at], preferred_element_type=jnp.float32)
                        for h in range(heads)
                    ]
                    ready = []
                    for h in range(heads):
                        masked = jnp.where(allowed, scores[h], NEG_FILL)
                        old = top[h]
                        new = jnp.maximum(old, jnp.max(masked, axis=0, keepdims=True))
                        weights = jnp.exp2((masked - new) * LOG2_SCALE)
                        factor = jnp.exp2((old - new) * LOG2_SCALE)
                        den[h] = den[h] * factor + jnp.sum(weights, axis=0, keepdims=True)
                        top[h] = new
                        ready.append((weights.astype(jnp.bfloat16), factor))
                    for h, (weights, factor) in enumerate(ready):
                        acc[h] = acc[h] * factor + jnp.dot(
                            turned_v[n, cols_of(h), take], weights, preferred_element_type=jnp.float32
                        )

        for h in range(heads):
            some = den[h] > 0.0
            safe = jnp.where(some, den[h], 1.0)
            lse = jnp.where(some, top[h] * LOG2_SCALE + jnp.log2(safe), NEG_FILL)
            finish(h, at, acc[h] / safe, lse)


def send_kernel(side, place, bounds, qa_ref, qb_ref, k_ref, v_ref, kv_ref, out_ref, *state):
    ctx = place[0] // HEADS_AXIS
    if side == 0:
        query_block, got_block = pick(ctx, 3, 2, 3, 0), pick(ctx, 1, 0, -1, -1)
        second, active = ctx == 2, ctx != 3
    else:
        query_block, got_block = pick(ctx, 1, 0, 3, 2), pick(ctx, -1, -1, 1, 0)
        second, active = ctx == 0, ctx != 1

    def finish(h, at, scaled, lse):
        out_ref[h, :HEAD_DIM, at] = scaled.astype(jnp.bfloat16)
        high = lse.astype(jnp.bfloat16).astype(jnp.float32)
        mid = (lse - high).astype(jnp.bfloat16).astype(jnp.float32)
        low = lse - high - mid
        line = lax.broadcasted_iota(jnp.int32, (EXTRA, SUB), 0)
        lines = jnp.where(line == 0, high, jnp.where(line == 1, mid, low))
        out_ref[h, HEAD_DIM:, at] = lines.astype(jnp.bfloat16)

    @pl.when(active)
    def _():
        query = jnp.where(second, qb_ref[...], qa_ref[...])
        sources = [
            (ctx, lambda h, take: k_ref[take, cols_of(h)], lambda: v_ref[...]),
            (got_block, lambda h, take: kv_ref[0, take, cols_of(h)], lambda: kv_ref[1]),
        ]
        fold_tiles(bounds, query_block, query, sources, SIDE, state, finish)


def keep_kernel(mode, place, bounds, q_ref, *rest):
    ctx = place[0] // HEADS_AXIS
    if mode is None:
        k_ref, v_ref, out_ref, lse_ref, *state = rest
        block, active = ctx, ctx >= 0
        source = (block, lambda h, take: k_ref[take, cols_of(h)], lambda: v_ref[...])
    else:
        kv_ref, out_ref, lse_ref, *state = rest
        block = pick(ctx, -1, 0, -1, -1) if mode == 0 else pick(ctx, -1, -1, 1, 0)
        active = block >= 0
        source = (block, lambda h, take: kv_ref[0, take, cols_of(h)], lambda: kv_ref[1])

    def finish(h, at, scaled, lse):
        out_ref[h, :, at] = scaled
        lse_ref[h, :, at] = jnp.broadcast_to(lse, (8, SUB))

    @pl.when(active)
    def _():
        fold_tiles(bounds, ctx, q_ref[...], [source], SIDE, state, finish)


def state_shapes(rows, sources):
    return [
        pltpu.VMEM((SIDE, 1, SUB), jnp.float32),
        pltpu.VMEM((SIDE, 1, SUB), jnp.float32),
        pltpu.VMEM((SIDE, HEAD_DIM, SUB), jnp.float32),
        pltpu.VMEM((SIDE * HEAD_DIM, rows), jnp.bfloat16),
        pltpu.VMEM((sources, SIDE * HEAD_DIM, rows), jnp.bfloat16),
    ]


def cost(rows, blocks, heads):
    return pl.CostEstimate(flops=1, bytes_accessed=1, transcendentals=0)


def fold_send(side, place, bounds, qa, qb, keys, values, got_kv):
    rows = keys.shape[0]
    half = SIDE * HEAD_DIM
    whole = pl.BlockSpec((rows, half), lambda i, *_: (0, 0))
    mine = pl.BlockSpec((rows, half), lambda i, *_: (0, side))
    return pl.pallas_call(
        functools.partial(send_kernel, side),
        out_shape=jax.ShapeDtypeStruct((SIDE, HEAD_DIM + EXTRA, rows), jnp.bfloat16),
        grid_spec=pltpu.PrefetchScalarGridSpec(
            num_scalar_prefetch=2,
            grid=(1,),
            in_specs=[whole, whole, mine, mine, pl.BlockSpec((2, rows, half), lambda i, *_: (0, 0, 0))],
            out_specs=pl.BlockSpec((SIDE, HEAD_DIM + EXTRA, rows), lambda i, *_: (0, 0, 0)),
            scratch_shapes=state_shapes(rows, 2),
        ),
        cost_estimate=cost(rows, 2, SIDE),
        name="fold_send",
    )(place, bounds, qa, qb, keys, values, got_kv)


def fold_keep(mode, place, bounds, queries, *pairs):
    rows, width = queries.shape
    half = SIDE * HEAD_DIM
    if mode is None:
        steps, spec = width // half, pl.BlockSpec((rows, half), lambda i, *_: (0, i))
        in_specs = [spec, spec, spec]
    else:
        steps = 1
        in_specs = [
            pl.BlockSpec((rows, half), lambda i, *_: (0, mode)),
            pl.BlockSpec((2, rows, half), lambda i, *_: (0, 0, 0)),
        ]
    return pl.pallas_call(
        functools.partial(keep_kernel, mode),
        out_shape=(
            jax.ShapeDtypeStruct((steps * SIDE, HEAD_DIM, rows), jnp.float32),
            jax.ShapeDtypeStruct((steps * SIDE, 8, rows), jnp.float32),
        ),
        grid_spec=pltpu.PrefetchScalarGridSpec(
            num_scalar_prefetch=2,
            grid=(steps,),
            in_specs=in_specs,
            out_specs=(
                pl.BlockSpec((SIDE, HEAD_DIM, rows), lambda i, *_: (i, 0, 0)),
                pl.BlockSpec((SIDE, 8, rows), lambda i, *_: (i, 0, 0)),
            ),
            scratch_shapes=state_shapes(rows, 1),
        ),
        cost_estimate=cost(rows, 1, steps * SIDE),
        name="fold_own" if mode is None else "fold_got",
    )(place, bounds, queries, *pairs)


def merge_kernel(place, own, own_lse, got_l, lse_l, got_r, lse_r, one_ref, two_ref, three_ref, out_ref):
    ctx = place[0] // HEADS_AXIS

    def sent(ref, flag, h):
        tail = ref[h, HEAD_DIM:, :].astype(jnp.float32)
        lse = jnp.where(flag, tail[0:1, :] + tail[1:2, :] + tail[2:3, :], NEG_FILL)
        return jnp.where(flag, ref[h, :HEAD_DIM, :].astype(jnp.float32), 0.0), lse

    def kept(ref, lse_ref, flag, h):
        return jnp.where(flag, ref[h], 0.0), jnp.where(flag, lse_ref[h, 0:1, :], NEG_FILL)

    def combine(others):
        for h in range(SIDE):
            parts = [(own[h], own_lse[h, 0:1, :])] + others(h)
            peak = functools.reduce(jnp.maximum, [lse for _, lse in parts])
            shares = [jnp.exp2(lse - peak) for _, lse in parts]
            inverse = 1.0 / functools.reduce(jnp.add, shares)
            summed = functools.reduce(jnp.add, [out * (share * inverse) for (out, _), share in zip(parts, shares)])
            out_ref[:, cols_of(h)] = summed.astype(out_ref.dtype).T

    @pl.when(pl.program_id(0) == 0)
    def _():
        combine(
            lambda h: [kept(got_l, lse_l, ctx == 1, h), sent(one_ref, ctx >= 2, h), sent(two_ref, ctx == 3, h)]
        )

    @pl.when(pl.program_id(0) == 1)
    def _():
        combine(lambda h: [kept(got_r, lse_r, ctx >= 2, h), sent(three_ref, ctx >= 1, h)])


def merge(place, own, got_l, got_r, one, two, three):
    rows = one.shape[2]
    tall = HEAD_DIM + EXTRA
    moving = lambda i, *_: (i, 0, 0)
    fixed = lambda i, *_: (0, 0, 0)
    pair = lambda at: [pl.BlockSpec((SIDE, HEAD_DIM, rows), at), pl.BlockSpec((SIDE, 8, rows), at)]
    return pl.pallas_call(
        merge_kernel,
        out_shape=jax.ShapeDtypeStruct((rows, 2 * SIDE * HEAD_DIM), jnp.bfloat16),
        grid_spec=pltpu.PrefetchScalarGridSpec(
            num_scalar_prefetch=1,
            grid=(2,),
            in_specs=pair(moving) + pair(fixed) + pair(fixed) + [pl.BlockSpec((SIDE, tall, rows), fixed)] * 3,
            out_specs=pl.BlockSpec((rows, SIDE * HEAD_DIM), lambda i, *_: (0, i)),
        ),
        name="merge",
    )(place, *own, *got_l, *got_r, one, two, three)


def on_device(mix_query, mix_key, mix_value, mr_filter, doc_ids, att_query, att_key, att_value):
    at_ctx = lax.axis_index("ctx")
    at_head = lax.axis_index("head")
    heads = lax.axis_size("head")
    blocks = lax.axis_size("ctx")
    half = SIDE * HEAD_DIM

    def pass_on(x, *pairs):
        return lax.ppermute(x, "ctx", list(pairs))

    pack_l = jnp.stack([att_key[:, :half], att_value[:, :half]])
    pack_r = jnp.stack([att_key[:, half:], att_value[:, half:]])
    query_l, query_r = att_query[:, :half], att_query[:, half:]
    query_x = jnp.where(at_ctx == 3, query_l, query_r)
    pack_l, pack_r, query_l, query_r, query_x, doc_ids, att_query = lax.optimization_barrier(
        (pack_l, pack_r, query_l, query_r, query_x, doc_ids, att_query)
    )
    kv_l = pass_on(pack_l, (0, 1), (1, 0))
    kv_r = pass_on(pack_r, (0, 3), (1, 2))
    q_x = pass_on(query_x, (3, 2), (1, 0))
    q_l = pass_on(query_l, (2, 1), (3, 0))
    q_r = pass_on(query_r, (2, 3), (3, 2))

    place = jnp.reshape(lax.axis_index(("ctx", "head")), (1,)).astype(jnp.int32)
    bounds = jnp.sum((doc_ids[None, :] < jnp.arange(4, dtype=jnp.int32)[:, None]).astype(jnp.int32), axis=1)

    own = fold_keep(None, place, bounds, att_query, att_key, att_value)
    product = (mix_key.astype(jnp.float32) * mix_value.astype(jnp.float32)).astype(jnp.bfloat16)
    own, q_x, q_l, q_r, kv_l, kv_r, product = lax.optimization_barrier((own, q_x, q_l, q_r, kv_l, kv_r, product))
    width = product.shape[1]
    count = blocks * heads
    prod_a, prod_b = product[:, : width // 2], product[:, width // 2 :]
    rim_a = lax.ppermute(prod_a, ("ctx", "head"), [(i, i + 1) for i in range(count - 1)])
    staged = lax.ppermute(
        prod_b, ("ctx", "head"), [(i, i + heads) for i in range(count - heads) if i % heads == heads - 1]
    )
    send_l = fold_send(0, place, bounds, q_l, q_x, att_key, att_value, kv_l)
    part_1 = pass_on(send_l, (1, 2), (0, 3))
    part_2 = pass_on(send_l, (2, 3))
    send_r = fold_send(1, place, bounds, q_r, q_x, att_key, att_value, kv_r)
    part_3 = pass_on(send_r, (0, 1), (3, 2), (2, 3))
    staged, prod_b, send_r, send_l, att_query = lax.optimization_barrier((staged, prod_b, send_r, send_l, att_query))
    rim_b = lax.ppermute(
        jnp.where(at_head == heads - 1, staged, prod_b), "head", [(i, (i + 1) % heads) for i in range(heads)]
    )
    got_l = fold_keep(0, place, bounds, att_query, kv_l)
    got_r = fold_keep(1, place, bounds, att_query, kv_r)
    mixed = mixer(place, bounds, rim_a, rim_b, product, mix_query, mr_filter)
    place, mixed = lax.optimization_barrier((place, mixed))
    attended = merge(place, own, got_l, got_r, part_1, part_2, part_3)
    return (mixed, attended)


def solution(mesh):
    placed = (
        P(("dp", "ctx", "head"), None),
        P(("dp", "ctx", "head"), None),
        P(("dp", "ctx", "head"), None),
        P(),
        P("dp"),
        P(("dp", "ctx"), "head"),
        P(("dp", "ctx"), "head"),
        P(("dp", "ctx"), "head"),
    )
    return jax.shard_map(
        on_device,
        mesh=mesh,
        in_specs=placed,
        out_specs=(P(("dp", "ctx", "head"), None), P(("dp", "ctx"), "head")),
        check_vma=False,
    )
```

```python
import functools
import math

import jax
import jax.numpy as jnp
from jax import lax
from jax.experimental import pallas as pl
from jax.experimental.pallas import tpu as pltpu
from jax.sharding import PartitionSpec as P

HEAD_DIM = 128
NEG_FILL = -1e30
LOG2_SCALE = math.log2(math.e) / math.sqrt(HEAD_DIM)
SIDE = 4
SUB = 256
EXTRA = 16
COLS = 2048
HEADS_AXIS = 4


def pick(at, *values):
    out = jnp.int32(values[-1])
    for i in range(len(values) - 2, -1, -1):
        out = jnp.where(at == i, jnp.int32(values[i]), out)
    return out


def first_of(bounds, position):
    first = jnp.zeros_like(position)
    for doc in range(1, 4):
        first = jnp.where(bounds[doc] <= position, bounds[doc], first)
    return first


def conv_kernel(group_size, place, bounds, rim_a_ref, rim_b_ref, prod_ref, query_ref, filt_ref, out_ref, mask):
    rows, cols = prod_ref.shape
    step = pl.program_id(0)

    @pl.when(step == 0)
    def _():
        token = place[0] * rows + lax.broadcasted_iota(jnp.int32, (2 * rows, rows), 1)
        source = (place[0] - 1) * rows + lax.broadcasted_iota(jnp.int32, (2 * rows, rows), 0)
        allowed = (source <= token) & (source > token - rows) & (source >= first_of(bounds, token))
        mask[...] = jnp.where(allowed, 1.0, 0.0).astype(jnp.bfloat16)

    rim = jnp.where(step < pl.num_programs(0) // 2, rim_a_ref[...], rim_b_ref[...])
    turned = jnp.concatenate([rim, prod_ref[...]], axis=0).T
    filters = filt_ref[...].astype(jnp.float32)
    allowed = mask[...]
    parts = []
    for g in range(cols // group_size):
        line = jnp.broadcast_to(filters[g : g + 1, :], (rows, rows))
        ring = pltpu.roll(line, 0, 1, stride=1, stride_axis=0).astype(jnp.bfloat16)
        taps = jnp.concatenate([ring, ring], axis=0) * allowed
        parts.append(
            jnp.dot(turned[g * group_size : (g + 1) * group_size], taps, preferred_element_type=jnp.float32)
        )
    total = jnp.concatenate(parts, axis=0).T
    out_ref[...] = (query_ref[...].astype(jnp.float32) * total).astype(out_ref.dtype)


def mixer(place, bounds, rim_a, rim_b, product, mix_query, mr_filter):
    rows, width = product.shape
    groups, filt_len = mr_filter.shape
    group_size = width // groups
    steps = width // COLS
    tile = pl.BlockSpec((rows, COLS), lambda i, *_: (0, i))
    return pl.pallas_call(
        functools.partial(conv_kernel, group_size),
        out_shape=jax.ShapeDtypeStruct((rows, width), jnp.bfloat16),
        grid_spec=pltpu.PrefetchScalarGridSpec(
            num_scalar_prefetch=2,
            grid=(steps,),
            in_specs=[
                pl.BlockSpec((rows, COLS), lambda i, *_: (0, jnp.minimum(i, steps // 2 - 1))),
                pl.BlockSpec((rows, COLS), lambda i, *_: (0, jnp.maximum(i - steps // 2, 0))),
                tile,
                tile,
                pl.BlockSpec((COLS // group_size, filt_len), lambda i, *_: (i, 0)),
            ],
            out_specs=tile,
            scratch_shapes=[pltpu.VMEM((2 * rows, rows), jnp.bfloat16)],
        ),
        cost_estimate=pl.CostEstimate(
            flops=2 * rows * 2 * filt_len * width * 16, bytes_accessed=8 * rows * width, transcendentals=0
        ),
        name="mixer",
    )(place, bounds, rim_a, rim_b, product, mix_query, mr_filter)


def cols_of(h):
    return slice(h * HEAD_DIM, (h + 1) * HEAD_DIM)


def fold_tiles(bounds, query_block, query, sources, heads, state, finish, tile=2 * SUB, turn=None):
    top, den, acc, turned_q, turned_v = state
    rows = query.shape[0]
    turned_q[...] = query.T
    whole_lowest = first_of(bounds, query_block * rows)
    for n, (block, _, value_of) in enumerate(sources):

        inside = (block >= 0) & (block <= query_block) & ((block + 1) * rows > whole_lowest)

        @pl.when(inside if turn is None else turn)
        def _(n=n, value_of=value_of):
            turned_v[n] = value_of().T

    for part in range(rows // SUB):
        at = pl.ds(part * SUB, SUB)
        query_from = query_block * rows + part * SUB
        line_pos = query_from + lax.broadcasted_iota(jnp.int32, (1, SUB), 1)
        first_row = first_of(bounds, line_pos)
        lowest = first_of(bounds, query_from)
        top[...] = jnp.full(top.shape, 0.5 * NEG_FILL, jnp.float32)
        den[...] = jnp.zeros(den.shape, jnp.float32)
        acc[...] = jnp.zeros(acc.shape, jnp.float32)
        for n, (block, key_of, _) in enumerate(sources):
            for piece in range(rows // tile):
                key_from = block * rows + piece * tile
                needed = (block >= 0) & (key_from <= query_from) & (key_from + tile > lowest)

                @pl.when(needed)
                def _(n=n, key_of=key_of, piece=piece, key_from=key_from):
                    take = pl.ds(piece * tile, tile)
                    key_pos = key_from + lax.broadcasted_iota(jnp.int32, (tile, SUB), 0)
                    allowed = (key_pos <= line_pos) & (key_pos >= first_row)
                    scores = [
                        jnp.dot(key_of(h, take), turned_q[cols_of(h), at], preferred_element_type=jnp.float32)
                        for h in range(heads)
                    ]
                    ready = []
                    for h in range(heads):
                        masked = jnp.where(allowed, scores[h], NEG_FILL)
                        old = top[h]
                        new = jnp.maximum(old, jnp.max(masked, axis=0, keepdims=True))
                        weights = jnp.exp2((masked - new) * LOG2_SCALE)
                        factor = jnp.exp2((old - new) * LOG2_SCALE)
                        den[h] = den[h] * factor + jnp.sum(weights, axis=0, keepdims=True)
                        top[h] = new
                        ready.append((weights.astype(jnp.bfloat16), factor))
                    for h, (weights, factor) in enumerate(ready):
                        acc[h] = acc[h] * factor + jnp.dot(
                            turned_v[n, cols_of(h), take], weights, preferred_element_type=jnp.float32
                        )

        for h in range(heads):
            some = den[h] > 0.0
            safe = jnp.where(some, den[h], 1.0)
            lse = jnp.where(some, top[h] * LOG2_SCALE + jnp.log2(safe), NEG_FILL)
            finish(h, at, acc[h] / safe, lse)


def write_message(out_ref, h, at, scaled, lse):
    out_ref[h, :HEAD_DIM, at] = scaled.astype(jnp.bfloat16)
    high = lse.astype(jnp.bfloat16).astype(jnp.float32)
    mid = (lse - high).astype(jnp.bfloat16).astype(jnp.float32)
    low = lse - high - mid
    line = lax.broadcasted_iota(jnp.int32, (EXTRA, SUB), 0)
    lines = jnp.where(line == 0, high, jnp.where(line == 1, mid, low))
    out_ref[h, HEAD_DIM:, at] = lines.astype(jnp.bfloat16)


def write_kept(out_ref, lse_ref, h, at, scaled, lse):
    out_ref[h, :, at] = scaled
    lse_ref[h, :, at] = jnp.broadcast_to(lse, (8, SUB))


def ctx_of(place):
    return place[0] // HEADS_AXIS


def late_side(place):
    return jnp.where(ctx_of(place) < 2, 0, 1)


def early_side(place):
    return jnp.where(ctx_of(place) == 0, 1, 0)


def own_source(block, k_ref, v_ref):
    return block, lambda h, take: k_ref[take, cols_of(h)], lambda: v_ref[...]


def fetch(place, left_ref, right_ref, held, sem):
    left = ctx_of(place) < 2

    @pl.when(left)
    def _():
        copy = pltpu.make_async_copy(left_ref, held, sem)
        copy.start()
        copy.wait()

    @pl.when(jnp.logical_not(left))
    def _():
        copy = pltpu.make_async_copy(right_ref, held, sem)
        copy.start()
        copy.wait()


def got_source(block, held):
    return block, lambda h, take: held[0, take, cols_of(h)], lambda: held[1]


def own_kernel(place, bounds, q_ref, k_ref, v_ref, out_ref, lse_ref, *state):
    ctx = ctx_of(place)
    finish = functools.partial(write_kept, out_ref, lse_ref)
    fold_tiles(bounds, ctx, q_ref[...], [own_source(ctx, k_ref, v_ref)], SIDE, state, finish, SUB)


def early_kernel(place, bounds, q_ref, k_ref, v_ref, out_ref, *state):
    ctx = ctx_of(place)

    @pl.when((ctx == 0) | (ctx == 2))
    def _():
        finish = functools.partial(write_message, out_ref)
        fold_tiles(bounds, ctx + 1, q_ref[...], [own_source(ctx, k_ref, v_ref)], SIDE, state, finish)


def carry_kernel(place, bounds, ql_ref, qr_ref, k_ref, v_ref, out_ref, lse_ref, *state):
    ctx = ctx_of(place)

    @pl.when(ctx < 3)
    def _():
        query = jnp.where(ctx < 2, ql_ref[...], qr_ref[...])
        finish = functools.partial(write_kept, out_ref, lse_ref)
        fold_tiles(
            bounds, pick(ctx, 3, 2, 3, 2), query, [own_source(ctx, k_ref, v_ref)], SIDE, state, finish
        )


def late_kernel(
    place, bounds, ql_ref, qr_ref, part_ref, part_lse, q_ref, left_ref, right_ref, out_ref, got_ref, got_lse,
    held, sem, *state
):
    ctx = ctx_of(place)
    fetch(place, left_ref, right_ref, held, sem)
    query = jnp.where(ctx < 2, ql_ref[...], qr_ref[...])
    carried = ctx < 3
    source = got_source(pick(ctx, 1, 0, 1, 0), held)

    def finish(h, at, scaled, lse):
        other = jnp.where(carried, part_lse[h, 0:1, at], NEG_FILL)
        before = jnp.where(carried, part_ref[h, :, at], 0.0)
        peak = jnp.maximum(lse, other)
        here, there = jnp.exp2(lse - peak), jnp.exp2(other - peak)
        both = here + there
        write_message(out_ref, h, at, (scaled * here + before * there) / both, peak + jnp.log2(both))

    fold_tiles(bounds, pick(ctx, 3, 2, 3, 2), query, [source], SIDE, state, finish, turn=ctx >= 0)

    @pl.when(ctx >= 1)
    def _():
        keep = functools.partial(write_kept, got_ref, got_lse)
        fold_tiles(bounds, ctx, q_ref[...], [source], SIDE, state, keep, turn=ctx < 0)


def fold_call(kernel, name, work, rows, steps, in_specs, message, got, arrays, place, bounds):
    half = SIDE * HEAD_DIM
    out_shape, out_specs = (), ()
    if message:
        out_shape = (jax.ShapeDtypeStruct((steps * SIDE, HEAD_DIM + EXTRA, rows), jnp.bfloat16),)
        out_specs = (pl.BlockSpec((SIDE, HEAD_DIM + EXTRA, rows), lambda i, *_: (i, 0, 0)),)
    if got or not message:
        out_shape += (
            jax.ShapeDtypeStruct((steps * SIDE, HEAD_DIM, rows), jnp.float32),
            jax.ShapeDtypeStruct((steps * SIDE, 8, rows), jnp.float32),
        )
        out_specs += (
            pl.BlockSpec((SIDE, HEAD_DIM, rows), lambda i, *_: (i, 0, 0)),
            pl.BlockSpec((SIDE, 8, rows), lambda i, *_: (i, 0, 0)),
        )
    scratch = [pltpu.VMEM((2, rows, half), jnp.bfloat16), pltpu.SemaphoreType.DMA] if got else []
    scratch += [
        pltpu.VMEM((SIDE, 1, SUB), jnp.float32),
        pltpu.VMEM((SIDE, 1, SUB), jnp.float32),
        pltpu.VMEM((SIDE, HEAD_DIM, SUB), jnp.float32),
        pltpu.VMEM((half, rows), jnp.bfloat16),
        pltpu.VMEM((1, half, rows), jnp.bfloat16),
    ]
    return pl.pallas_call(
        kernel,
        out_shape=out_shape,
        grid_spec=pltpu.PrefetchScalarGridSpec(
            num_scalar_prefetch=2, grid=(steps,), in_specs=in_specs, out_specs=out_specs, scratch_shapes=scratch
        ),
        cost_estimate=pl.CostEstimate(flops=work, bytes_accessed=1, transcendentals=0),
        name=name,
    )(place, bounds, *arrays)


def pack_kernel(place, q_ref, k_ref, v_ref, left, right, q_l, q_r, q_x, held, in_sems, out_sems):
    half = SIDE * HEAD_DIM
    low, high = pl.ds(0, half), pl.ds(half, half)
    reads = [
        pltpu.make_async_copy(ref.at[:, cols], held.at[n], in_sems.at[n])
        for n, (ref, cols) in enumerate(
            [(k_ref, low), (v_ref, low), (k_ref, high), (v_ref, high), (q_ref, low), (q_ref, high)]
        )
    ]
    writes = [
        pltpu.make_async_copy(held.at[0:2], left, out_sems.at[0]),
        pltpu.make_async_copy(held.at[2:4], right, out_sems.at[1]),
        pltpu.make_async_copy(held.at[4], q_l, out_sems.at[2]),
        pltpu.make_async_copy(held.at[5], q_r, out_sems.at[3]),
        pltpu.make_async_copy(held.at[jnp.where(ctx_of(place) == 3, 4, 5)], q_x, out_sems.at[4]),
    ]
    for copy in reads:
        copy.start()
    for n, copy in enumerate(reads):
        copy.wait()
        for ready in {1: [0], 3: [1], 4: [2], 5: [3, 4]}.get(n, []):
            writes[ready].start()
    for copy in writes:
        copy.wait()


def pack(place, queries, keys, values):
    rows = keys.shape[0]
    half = SIDE * HEAD_DIM
    anywhere = pl.BlockSpec(memory_space=pl.ANY)
    both = jax.ShapeDtypeStruct((2, rows, half), jnp.bfloat16)
    single = jax.ShapeDtypeStruct((rows, half), jnp.bfloat16)
    return pl.pallas_call(
        pack_kernel,
        out_shape=(both, both, single, single, single),
        grid_spec=pltpu.PrefetchScalarGridSpec(
            num_scalar_prefetch=1,
            grid=(1,),
            in_specs=[anywhere] * 3,
            out_specs=[anywhere] * 5,
            scratch_shapes=[
                pltpu.VMEM((6, rows, half), jnp.bfloat16),
                pltpu.SemaphoreType.DMA((6,)),
                pltpu.SemaphoreType.DMA((5,)),
            ],
        ),
        name="pack",
    )(place, queries, keys, values)


def merge_kernel(place, own, own_lse, got, got_lse, one_ref, two_ref, three_ref, out_ref):
    ctx = ctx_of(place)

    def sent(ref, flag, h):
        tail = ref[h, HEAD_DIM:, :].astype(jnp.float32)
        lse = jnp.where(flag, tail[0:1, :] + tail[1:2, :] + tail[2:3, :], NEG_FILL)
        return jnp.where(flag, ref[h, :HEAD_DIM, :].astype(jnp.float32), 0.0), lse

    def kept(ref, lse_ref, flag, h):
        return jnp.where(flag, ref[h], 0.0), jnp.where(flag, lse_ref[h, 0:1, :], NEG_FILL)

    def combine(others):
        for h in range(SIDE):
            parts = [(own[h], own_lse[h, 0:1, :])] + others(h)
            peak = functools.reduce(jnp.maximum, [lse for _, lse in parts])
            shares = [jnp.exp2(lse - peak) for _, lse in parts]
            inverse = 1.0 / functools.reduce(jnp.add, shares)
            summed = functools.reduce(jnp.add, [out * (share * inverse) for (out, _), share in zip(parts, shares)])
            out_ref[:, cols_of(h)] = summed.astype(out_ref.dtype).T

    @pl.when(pl.program_id(0) == 0)
    def _():
        combine(
            lambda h: [kept(got, got_lse, ctx == 1, h), sent(one_ref, ctx >= 2, h), sent(three_ref, ctx == 3, h)]
        )

    @pl.when(pl.program_id(0) == 1)
    def _():
        combine(
            lambda h: [kept(got, got_lse, ctx >= 2, h), sent(two_ref, ctx >= 2, h), sent(three_ref, ctx == 1, h)]
        )


def merge(place, own, got, one, two, three):
    rows = one.shape[2]
    tall = HEAD_DIM + EXTRA
    moving = lambda i, *_: (i, 0, 0)
    fixed = lambda i, *_: (0, 0, 0)
    pair = lambda at: [pl.BlockSpec((SIDE, HEAD_DIM, rows), at), pl.BlockSpec((SIDE, 8, rows), at)]
    return pl.pallas_call(
        merge_kernel,
        out_shape=jax.ShapeDtypeStruct((rows, 2 * SIDE * HEAD_DIM), jnp.bfloat16),
        grid_spec=pltpu.PrefetchScalarGridSpec(
            num_scalar_prefetch=1,
            grid=(2,),
            in_specs=pair(moving) + pair(fixed) + [pl.BlockSpec((SIDE, tall, rows), fixed)] * 3,
            out_specs=pl.BlockSpec((rows, SIDE * HEAD_DIM), lambda i, *_: (0, i)),
        ),
        name="merge",
    )(place, *own, *got, one, two, three)


def on_device(mix_query, mix_key, mix_value, mr_filter, doc_ids, att_query, att_key, att_value):
    at_head = lax.axis_index("head")
    heads = lax.axis_size("head")
    blocks = lax.axis_size("ctx")
    half = SIDE * HEAD_DIM
    rows = att_key.shape[0]

    def pass_on(x, *pairs):
        return lax.ppermute(x, "ctx", list(pairs))

    place = jnp.reshape(lax.axis_index(("ctx", "head")), (1,)).astype(jnp.int32)
    pack_l, pack_r, query_l, query_r, query_x = pack(place, att_query, att_key, att_value)
    pack_l, pack_r, query_l, query_r, query_x, doc_ids, att_query, mix_key = lax.optimization_barrier(
        (pack_l, pack_r, query_l, query_r, query_x, doc_ids, att_query, mix_key)
    )
    kv_l = pass_on(pack_l, (0, 1), (1, 0))
    kv_r = pass_on(pack_r, (0, 3), (1, 2))
    q_x = pass_on(query_x, (3, 2), (1, 0))
    q_l = pass_on(query_l, (2, 1), (3, 0))
    q_r = pass_on(query_r, (2, 3), (3, 2))
    bounds = jnp.sum((doc_ids[None, :] < jnp.arange(4, dtype=jnp.int32)[:, None]).astype(jnp.int32), axis=1)

    product = (mix_key.astype(jnp.float32) * mix_value.astype(jnp.float32)).astype(jnp.bfloat16)
    width = product.shape[1]
    count = blocks * heads

    whole = pl.BlockSpec((rows, half), lambda i, *_: (0, 0))
    stepped = pl.BlockSpec((rows, half), lambda i, *_: (0, i))
    at_early = pl.BlockSpec((rows, half), lambda i, place, bounds: (0, early_side(place)))
    at_late = pl.BlockSpec((rows, half), lambda i, place, bounds: (0, late_side(place)))
    anywhere = pl.BlockSpec(memory_space=pl.ANY)
    part = [
        pl.BlockSpec((SIDE, HEAD_DIM, rows), lambda i, *_: (0, 0, 0)),
        pl.BlockSpec((SIDE, 8, rows), lambda i, *_: (0, 0, 0)),
    ]

    own = fold_call(
        own_kernel, "fold_own", 1, rows, 2, [stepped] * 3, False, False,
        (att_query, att_key, att_value), place, bounds,
    )
    own, q_x, q_l, q_r, product = lax.optimization_barrier((own, q_x, q_l, q_r, product))
    (early,) = fold_call(
        early_kernel, "fold_early", 1, rows, 1, [whole, at_early, at_early], True, False,
        (q_x, att_key, att_value), place, bounds,
    )
    part_3 = pass_on(early, (0, 1), (2, 3))
    q_l, q_r, early = lax.optimization_barrier((q_l, q_r, early))
    carry = fold_call(
        carry_kernel, "fold_carry", 1, rows, 1, [whole, whole, at_late, at_late], False, False,
        (q_l, q_r, att_key, att_value), place, bounds,
    )
    carry, kv_l, kv_r, product = lax.optimization_barrier((carry, kv_l, kv_r, product))
    prod_a, prod_b = product[:, : width // 2], product[:, width // 2 :]
    rim_a = lax.ppermute(prod_a, ("ctx", "head"), [(i, i + 1) for i in range(count - 1)])
    staged = lax.ppermute(
        prod_b, ("ctx", "head"), [(i, i + heads) for i in range(count - heads) if i % heads == heads - 1]
    )
    late, *got = fold_call(
        late_kernel, "fold_late", 1, rows, 1, [whole, whole, *part, at_late, anywhere, anywhere], True, True,
        (q_l, q_r, *carry, att_query, kv_l, kv_r), place, bounds,
    )
    part_1 = pass_on(late, (0, 3), (1, 2))
    part_2 = pass_on(late, (2, 3), (3, 2))
    staged, prod_b, late, got = lax.optimization_barrier((staged, prod_b, late, got))
    rim_b = lax.ppermute(
        jnp.where(at_head == heads - 1, staged, prod_b), "head", [(i, (i + 1) % heads) for i in range(heads)]
    )
    mixed = mixer(place, bounds, rim_a, rim_b, product, mix_query, mr_filter)
    place, mixed = lax.optimization_barrier((place, mixed))
    attended = merge(place, own, got, part_1, part_2, part_3)
    return (mixed, attended)


def solution(mesh):
    placed = (
        P(("dp", "ctx", "head"), None),
        P(("dp", "ctx", "head"), None),
        P(("dp", "ctx", "head"), None),
        P(),
        P("dp"),
        P(("dp", "ctx"), "head"),
        P(("dp", "ctx"), "head"),
        P(("dp", "ctx"), "head"),
    )
    return jax.shard_map(
        on_device,
        mesh=mesh,
        in_specs=placed,
        out_specs=(P(("dp", "ctx", "head"), None), P(("dp", "ctx"), "head")),
        check_vma=False,
    )
```

```python
import functools
import math

import jax
import jax.numpy as jnp
from jax import lax
from jax.experimental import pallas as pl
from jax.experimental.pallas import tpu as pltpu
from jax.sharding import PartitionSpec as P

HEAD_DIM = 128
NEG_FILL = -1e30
LOG2_SCALE = math.log2(math.e) / math.sqrt(HEAD_DIM)
SIDE = 4
SUB = 256
EXTRA = 8
COLS = 2048
HEADS_AXIS = 4


def pick(at, *values):
    out = jnp.int32(values[-1])
    for i in range(len(values) - 2, -1, -1):
        out = jnp.where(at == i, jnp.int32(values[i]), out)
    return out


def first_of(bounds, position):
    first = jnp.zeros_like(position)
    for doc in range(1, 4):
        first = jnp.where(bounds[doc] <= position, bounds[doc], first)
    return first


def conv_kernel(group_size, place, bounds, rim_a_ref, rim_b_ref, prod_ref, query_ref, filt_ref, out_ref, mask):
    rows, cols = prod_ref.shape
    step = pl.program_id(0)

    @pl.when(step == 0)
    def _():
        token = place[0] * rows + lax.broadcasted_iota(jnp.int32, (2 * rows, rows), 1)
        source = (place[0] - 1) * rows + lax.broadcasted_iota(jnp.int32, (2 * rows, rows), 0)
        allowed = (source <= token) & (source > token - rows) & (source >= first_of(bounds, token))
        mask[...] = jnp.where(allowed, 1.0, 0.0).astype(jnp.bfloat16)

    rim = jnp.where(step < pl.num_programs(0) // 2, rim_a_ref[...], rim_b_ref[...])
    turned = jnp.concatenate([rim, prod_ref[...]], axis=0).T
    filters = filt_ref[...].astype(jnp.float32)
    allowed = mask[...]
    parts = []
    for g in range(cols // group_size):
        line = jnp.broadcast_to(filters[g : g + 1, :], (rows, rows))
        ring = pltpu.roll(line, 0, 1, stride=1, stride_axis=0).astype(jnp.bfloat16)
        taps = jnp.concatenate([ring, ring], axis=0) * allowed
        parts.append(
            jnp.dot(turned[g * group_size : (g + 1) * group_size], taps, preferred_element_type=jnp.float32)
        )
    total = jnp.concatenate(parts, axis=0).T
    out_ref[...] = (query_ref[...].astype(jnp.float32) * total).astype(out_ref.dtype)


def mixer(place, bounds, rim_a, rim_b, product, mix_query, mr_filter):
    rows, width = product.shape
    groups, filt_len = mr_filter.shape
    group_size = width // groups
    steps = width // COLS
    tile = pl.BlockSpec((rows, COLS), lambda i, *_: (0, i))
    return pl.pallas_call(
        functools.partial(conv_kernel, group_size),
        out_shape=jax.ShapeDtypeStruct((rows, width), jnp.bfloat16),
        grid_spec=pltpu.PrefetchScalarGridSpec(
            num_scalar_prefetch=2,
            grid=(steps,),
            in_specs=[
                pl.BlockSpec((rows, COLS), lambda i, *_: (0, jnp.minimum(i, steps // 2 - 1))),
                pl.BlockSpec((rows, COLS), lambda i, *_: (0, jnp.maximum(i - steps // 2, 0))),
                tile,
                tile,
                pl.BlockSpec((COLS // group_size, filt_len), lambda i, *_: (i, 0)),
            ],
            out_specs=tile,
            scratch_shapes=[pltpu.VMEM((2 * rows, rows), jnp.bfloat16)],
        ),
        cost_estimate=pl.CostEstimate(
            flops=2 * rows * 2 * filt_len * width * 16, bytes_accessed=8 * rows * width, transcendentals=0
        ),
        name="mixer",
    )(place, bounds, rim_a, rim_b, product, mix_query, mr_filter)


def cols_of(h):
    return slice(h * HEAD_DIM, (h + 1) * HEAD_DIM)


def fold_tiles(bounds, query_block, query, sources, heads, state, finish, tile=2 * SUB, turn=None):
    top, den, acc, turned_q, turned_v = state
    rows = query.shape[0]
    turned_q[...] = query.T
    whole_lowest = first_of(bounds, query_block * rows)
    for n, (block, _, value_of) in enumerate(sources):

        inside = (block >= 0) & (block <= query_block) & ((block + 1) * rows > whole_lowest)

        @pl.when(inside if turn is None else turn)
        def _(n=n, value_of=value_of):
            turned_v[n] = value_of().T

    for part in range(rows // SUB):
        at = pl.ds(part * SUB, SUB)
        query_from = query_block * rows + part * SUB
        line_pos = query_from + lax.broadcasted_iota(jnp.int32, (1, SUB), 1)
        first_row = first_of(bounds, line_pos)
        lowest = first_of(bounds, query_from)
        top[...] = jnp.full(top.shape, 0.5 * NEG_FILL, jnp.float32)
        den[...] = jnp.zeros(den.shape, jnp.float32)
        acc[...] = jnp.zeros(acc.shape, jnp.float32)
        for n, (block, key_of, _) in enumerate(sources):
            for piece in range(rows // tile):
                key_from = block * rows + piece * tile
                needed = (block >= 0) & (key_from <= query_from) & (key_from + tile > lowest)

                @pl.when(needed)
                def _(n=n, key_of=key_of, piece=piece, key_from=key_from):
                    take = pl.ds(piece * tile, tile)
                    key_pos = key_from + lax.broadcasted_iota(jnp.int32, (tile, SUB), 0)
                    allowed = (key_pos <= line_pos) & (key_pos >= first_row)
                    scores = [
                        jnp.dot(key_of(h, take), turned_q[cols_of(h), at], preferred_element_type=jnp.float32)
                        for h in range(heads)
                    ]
                    ready = []
                    for h in range(heads):
                        masked = jnp.where(allowed, scores[h], NEG_FILL)
                        old = top[h]
                        new = jnp.maximum(old, jnp.max(masked, axis=0, keepdims=True))
                        weights = jnp.exp2((masked - new) * LOG2_SCALE)
                        factor = jnp.exp2((old - new) * LOG2_SCALE)
                        den[h] = den[h] * factor + jnp.sum(weights, axis=0, keepdims=True)
                        top[h] = new
                        ready.append((weights.astype(jnp.bfloat16), factor))
                    for h, (weights, factor) in enumerate(ready):
                        acc[h] = acc[h] * factor + jnp.dot(
                            turned_v[n, cols_of(h), take], weights, preferred_element_type=jnp.float32
                        )

        for h in range(heads):
            some = den[h] > 0.0
            safe = jnp.where(some, den[h], 1.0)
            lse = jnp.where(some, top[h] * LOG2_SCALE + jnp.log2(safe), NEG_FILL)
            finish(h, at, acc[h] / safe, lse)


def write_message(out_ref, h, at, scaled, lse):
    out_ref[h, :HEAD_DIM, at] = scaled.astype(jnp.bfloat16)
    high = lse.astype(jnp.bfloat16).astype(jnp.float32)
    mid = (lse - high).astype(jnp.bfloat16).astype(jnp.float32)
    low = lse - high - mid
    line = lax.broadcasted_iota(jnp.int32, (EXTRA, SUB), 0)
    lines = jnp.where(line == 0, high, jnp.where(line == 1, mid, low))
    out_ref[h, HEAD_DIM:, at] = lines.astype(jnp.bfloat16)


def write_kept(out_ref, lse_ref, h, at, scaled, lse):
    out_ref[h, :, at] = scaled
    lse_ref[h, :, at] = jnp.broadcast_to(lse, (8, SUB))


def ctx_of(place):
    return place[0] // HEADS_AXIS


def late_side(place):
    return jnp.where(ctx_of(place) < 2, 0, 1)


def early_side(place):
    return jnp.where(ctx_of(place) == 0, 1, 0)


def own_source(block, k_ref, v_ref):
    return block, lambda h, take: k_ref[take, cols_of(h)], lambda: v_ref[...]


def fetch(place, left_ref, right_ref, held, sem):
    left = ctx_of(place) < 2

    @pl.when(left)
    def _():
        copy = pltpu.make_async_copy(left_ref, held, sem)
        copy.start()
        copy.wait()

    @pl.when(jnp.logical_not(left))
    def _():
        copy = pltpu.make_async_copy(right_ref, held, sem)
        copy.start()
        copy.wait()


def got_source(block, held):
    return block, lambda h, take: held[0, take, cols_of(h)], lambda: held[1]


def own_kernel(place, bounds, q_ref, k_ref, v_ref, out_ref, lse_ref, *state):
    ctx = ctx_of(place)
    finish = functools.partial(write_kept, out_ref, lse_ref)
    fold_tiles(bounds, ctx, q_ref[...], [own_source(ctx, k_ref, v_ref)], SIDE, state, finish, SUB)


def early_kernel(place, bounds, q_ref, k_ref, v_ref, out_ref, *state):
    ctx = ctx_of(place)

    @pl.when((ctx == 0) | (ctx == 2))
    def _():
        finish = functools.partial(write_message, out_ref)
        fold_tiles(bounds, ctx + 1, q_ref[...], [own_source(ctx, k_ref, v_ref)], SIDE, state, finish)


def carry_kernel(place, bounds, ql_ref, qr_ref, k_ref, v_ref, out_ref, lse_ref, *state):
    ctx = ctx_of(place)

    @pl.when(ctx < 3)
    def _():
        query = jnp.where(ctx < 2, ql_ref[...], qr_ref[...])
        finish = functools.partial(write_kept, out_ref, lse_ref)
        fold_tiles(
            bounds, pick(ctx, 3, 2, 3, 2), query, [own_source(ctx, k_ref, v_ref)], SIDE, state, finish
        )


def late_kernel(
    place, bounds, ql_ref, qr_ref, part_ref, part_lse, q_ref, left_ref, right_ref, out_ref, got_ref, got_lse,
    held, sem, *state
):
    ctx = ctx_of(place)
    fetch(place, left_ref, right_ref, held, sem)
    query = jnp.where(ctx < 2, ql_ref[...], qr_ref[...])
    carried = ctx < 3
    source = got_source(pick(ctx, 1, 0, 1, 0), held)

    def finish(h, at, scaled, lse):
        other = jnp.where(carried, part_lse[h, 0:1, at], NEG_FILL)
        before = jnp.where(carried, part_ref[h, :, at], 0.0)
        peak = jnp.maximum(lse, other)
        here, there = jnp.exp2(lse - peak), jnp.exp2(other - peak)
        both = here + there
        write_message(out_ref, h, at, (scaled * here + before * there) / both, peak + jnp.log2(both))

    fold_tiles(bounds, pick(ctx, 3, 2, 3, 2), query, [source], SIDE, state, finish, turn=ctx >= 0)

    @pl.when(ctx >= 1)
    def _():
        keep = functools.partial(write_kept, got_ref, got_lse)
        fold_tiles(bounds, ctx, q_ref[...], [source], SIDE, state, keep, turn=ctx < 0)


def fold_call(kernel, name, work, rows, steps, in_specs, message, got, arrays, place, bounds):
    half = SIDE * HEAD_DIM
    out_shape, out_specs = (), ()
    if message:
        out_shape = (jax.ShapeDtypeStruct((steps * SIDE, HEAD_DIM + EXTRA, rows), jnp.bfloat16),)
        out_specs = (pl.BlockSpec((SIDE, HEAD_DIM + EXTRA, rows), lambda i, *_: (i, 0, 0)),)
    if got or not message:
        out_shape += (
            jax.ShapeDtypeStruct((steps * SIDE, HEAD_DIM, rows), jnp.float32),
            jax.ShapeDtypeStruct((steps * SIDE, 8, rows), jnp.float32),
        )
        out_specs += (
            pl.BlockSpec((SIDE, HEAD_DIM, rows), lambda i, *_: (i, 0, 0)),
            pl.BlockSpec((SIDE, 8, rows), lambda i, *_: (i, 0, 0)),
        )
    scratch = [pltpu.VMEM((2, rows, half), jnp.bfloat16), pltpu.SemaphoreType.DMA] if got else []
    scratch += [
        pltpu.VMEM((SIDE, 1, SUB), jnp.float32),
        pltpu.VMEM((SIDE, 1, SUB), jnp.float32),
        pltpu.VMEM((SIDE, HEAD_DIM, SUB), jnp.float32),
        pltpu.VMEM((half, rows), jnp.bfloat16),
        pltpu.VMEM((1, half, rows), jnp.bfloat16),
    ]
    return pl.pallas_call(
        kernel,
        out_shape=out_shape,
        grid_spec=pltpu.PrefetchScalarGridSpec(
            num_scalar_prefetch=2, grid=(steps,), in_specs=in_specs, out_specs=out_specs, scratch_shapes=scratch
        ),
        cost_estimate=pl.CostEstimate(flops=work, bytes_accessed=1, transcendentals=0),
        name=name,
    )(place, bounds, *arrays)


def pack_kernel(place, q_ref, k_ref, v_ref, left, right, q_l, q_r, q_x, held, in_sems, out_sems):
    half = SIDE * HEAD_DIM
    low, high = pl.ds(0, half), pl.ds(half, half)
    reads = [
        pltpu.make_async_copy(ref.at[:, cols], held.at[n], in_sems.at[n])
        for n, (ref, cols) in enumerate(
            [(k_ref, low), (v_ref, low), (k_ref, high), (v_ref, high), (q_ref, low), (q_ref, high)]
        )
    ]
    writes = [
        pltpu.make_async_copy(held.at[0:2], left, out_sems.at[0]),
        pltpu.make_async_copy(held.at[2:4], right, out_sems.at[1]),
        pltpu.make_async_copy(held.at[4], q_l, out_sems.at[2]),
        pltpu.make_async_copy(held.at[5], q_r, out_sems.at[3]),
        pltpu.make_async_copy(held.at[jnp.where(ctx_of(place) == 3, 4, 5)], q_x, out_sems.at[4]),
    ]
    for copy in reads:
        copy.start()
    for n, copy in enumerate(reads):
        copy.wait()
        for ready in {1: [0], 3: [1], 4: [2], 5: [3, 4]}.get(n, []):
            writes[ready].start()
    for copy in writes:
        copy.wait()


def pack(place, queries, keys, values):
    rows = keys.shape[0]
    half = SIDE * HEAD_DIM
    anywhere = pl.BlockSpec(memory_space=pl.ANY)
    both = jax.ShapeDtypeStruct((2, rows, half), jnp.bfloat16)
    single = jax.ShapeDtypeStruct((rows, half), jnp.bfloat16)
    return pl.pallas_call(
        pack_kernel,
        out_shape=(both, both, single, single, single),
        grid_spec=pltpu.PrefetchScalarGridSpec(
            num_scalar_prefetch=1,
            grid=(1,),
            in_specs=[anywhere] * 3,
            out_specs=[anywhere] * 5,
            scratch_shapes=[
                pltpu.VMEM((6, rows, half), jnp.bfloat16),
                pltpu.SemaphoreType.DMA((6,)),
                pltpu.SemaphoreType.DMA((5,)),
            ],
        ),
        name="pack",
    )(place, queries, keys, values)


def merge_kernel(place, own, own_lse, got, got_lse, one_ref, two_ref, three_ref, out_ref):
    ctx = ctx_of(place)

    def sent(ref, flag, h):
        tail = ref[h, HEAD_DIM:, :].astype(jnp.float32)
        lse = jnp.where(flag, tail[0:1, :] + tail[1:2, :] + tail[2:3, :], NEG_FILL)
        return jnp.where(flag, ref[h, :HEAD_DIM, :].astype(jnp.float32), 0.0), lse

    def kept(ref, lse_ref, flag, h):
        return jnp.where(flag, ref[h], 0.0), jnp.where(flag, lse_ref[h, 0:1, :], NEG_FILL)

    def combine(others):
        for h in range(SIDE):
            parts = [(own[h], own_lse[h, 0:1, :])] + others(h)
            peak = functools.reduce(jnp.maximum, [lse for _, lse in parts])
            shares = [jnp.exp2(lse - peak) for _, lse in parts]
            inverse = 1.0 / functools.reduce(jnp.add, shares)
            summed = functools.reduce(jnp.add, [out * (share * inverse) for (out, _), share in zip(parts, shares)])
            out_ref[:, cols_of(h)] = summed.astype(out_ref.dtype).T

    @pl.when(pl.program_id(0) == 0)
    def _():
        combine(
            lambda h: [kept(got, got_lse, ctx == 1, h), sent(one_ref, ctx >= 2, h), sent(three_ref, ctx == 3, h)]
        )

    @pl.when(pl.program_id(0) == 1)
    def _():
        combine(
            lambda h: [kept(got, got_lse, ctx >= 2, h), sent(two_ref, ctx >= 2, h), sent(three_ref, ctx == 1, h)]
        )


def merge(place, own, got, one, two, three):
    rows = one.shape[2]
    tall = HEAD_DIM + EXTRA
    moving = lambda i, *_: (i, 0, 0)
    fixed = lambda i, *_: (0, 0, 0)
    pair = lambda at: [pl.BlockSpec((SIDE, HEAD_DIM, rows), at), pl.BlockSpec((SIDE, 8, rows), at)]
    return pl.pallas_call(
        merge_kernel,
        out_shape=jax.ShapeDtypeStruct((rows, 2 * SIDE * HEAD_DIM), jnp.bfloat16),
        grid_spec=pltpu.PrefetchScalarGridSpec(
            num_scalar_prefetch=1,
            grid=(2,),
            in_specs=pair(moving) + pair(fixed) + [pl.BlockSpec((SIDE, tall, rows), fixed)] * 3,
            out_specs=pl.BlockSpec((rows, SIDE * HEAD_DIM), lambda i, *_: (0, i)),
        ),
        name="merge",
    )(place, *own, *got, one, two, three)


def on_device(mix_query, mix_key, mix_value, mr_filter, doc_ids, att_query, att_key, att_value):
    at_head = lax.axis_index("head")
    heads = lax.axis_size("head")
    blocks = lax.axis_size("ctx")
    half = SIDE * HEAD_DIM
    rows = att_key.shape[0]

    def pass_on(x, *pairs):
        return lax.ppermute(x, "ctx", list(pairs))

    place = jnp.reshape(lax.axis_index(("ctx", "head")), (1,)).astype(jnp.int32)
    pack_l, pack_r, query_l, query_r, query_x = pack(place, att_query, att_key, att_value)
    pack_l, pack_r, query_l, query_r, query_x, doc_ids, att_query, mix_key = lax.optimization_barrier(
        (pack_l, pack_r, query_l, query_r, query_x, doc_ids, att_query, mix_key)
    )
    kv_l = pass_on(pack_l, (0, 1), (1, 0))
    kv_r = pass_on(pack_r, (0, 3), (1, 2))
    q_x = pass_on(query_x, (3, 2), (1, 0))
    q_l = pass_on(query_l, (2, 1), (3, 0))
    q_r = pass_on(query_r, (2, 3), (3, 2))
    bounds = jnp.sum((doc_ids[None, :] < jnp.arange(4, dtype=jnp.int32)[:, None]).astype(jnp.int32), axis=1)

    product = (mix_key.astype(jnp.float32) * mix_value.astype(jnp.float32)).astype(jnp.bfloat16)
    width = product.shape[1]
    count = blocks * heads

    whole = pl.BlockSpec((rows, half), lambda i, *_: (0, 0))
    stepped = pl.BlockSpec((rows, half), lambda i, *_: (0, i))
    at_early = pl.BlockSpec((rows, half), lambda i, place, bounds: (0, early_side(place)))
    at_late = pl.BlockSpec((rows, half), lambda i, place, bounds: (0, late_side(place)))
    anywhere = pl.BlockSpec(memory_space=pl.ANY)
    part = [
        pl.BlockSpec((SIDE, HEAD_DIM, rows), lambda i, *_: (0, 0, 0)),
        pl.BlockSpec((SIDE, 8, rows), lambda i, *_: (0, 0, 0)),
    ]

    own = fold_call(
        own_kernel, "fold_own", 1, rows, 2, [stepped] * 3, False, False,
        (att_query, att_key, att_value), place, bounds,
    )
    own, q_x, q_l, q_r, product = lax.optimization_barrier((own, q_x, q_l, q_r, product))
    (early,) = fold_call(
        early_kernel, "fold_early", 1, rows, 1, [whole, at_early, at_early], True, False,
        (q_x, att_key, att_value), place, bounds,
    )
    part_3 = pass_on(early, (0, 1), (2, 3))
    q_l, q_r, early = lax.optimization_barrier((q_l, q_r, early))
    carry = fold_call(
        carry_kernel, "fold_carry", 1, rows, 1, [whole, whole, at_late, at_late], False, False,
        (q_l, q_r, att_key, att_value), place, bounds,
    )
    carry, kv_l, kv_r, product = lax.optimization_barrier((carry, kv_l, kv_r, product))
    prod_a, prod_b = product[:, : width // 2], product[:, width // 2 :]
    rim_a = lax.ppermute(prod_a, ("ctx", "head"), [(i, i + 1) for i in range(count - 1)])
    staged = lax.ppermute(
        prod_b, ("ctx", "head"), [(i, i + heads) for i in range(count - heads) if i % heads == heads - 1]
    )
    late, *got = fold_call(
        late_kernel, "fold_late", 1, rows, 1, [whole, whole, *part, at_late, anywhere, anywhere], True, True,
        (q_l, q_r, *carry, att_query, kv_l, kv_r), place, bounds,
    )
    part_1 = pass_on(late, (0, 3), (1, 2))
    part_2 = pass_on(late, (2, 3), (3, 2))
    staged, prod_b, late, got = lax.optimization_barrier((staged, prod_b, late, got))
    rim_b = lax.ppermute(
        jnp.where(at_head == heads - 1, staged, prod_b), "head", [(i, (i + 1) % heads) for i in range(heads)]
    )
    mixed = mixer(place, bounds, rim_a, rim_b, product, mix_query, mr_filter)
    place, mixed = lax.optimization_barrier((place, mixed))
    attended = merge(place, own, got, part_1, part_2, part_3)
    return (mixed, attended)


def solution(mesh):
    placed = (
        P(("dp", "ctx", "head"), None),
        P(("dp", "ctx", "head"), None),
        P(("dp", "ctx", "head"), None),
        P(),
        P("dp"),
        P(("dp", "ctx"), "head"),
        P(("dp", "ctx"), "head"),
        P(("dp", "ctx"), "head"),
    )
    return jax.shard_map(
        on_device,
        mesh=mesh,
        in_specs=placed,
        out_specs=(P(("dp", "ctx", "head"), None), P(("dp", "ctx"), "head")),
        check_vma=False,
    )
```

```python
import functools
import math

import jax
import jax.numpy as jnp
from jax import lax
from jax.experimental import pallas as pl
from jax.experimental.pallas import tpu as pltpu
from jax.sharding import PartitionSpec as P

HEAD_DIM = 128
NEG_FILL = -1e30
LOG2_SCALE = math.log2(math.e) / math.sqrt(HEAD_DIM)
SIDE = 4
SUB = 256
EXTRA = 8
COLS = 4096
HEADS_AXIS = 4


def pick(at, *values):
    out = jnp.int32(values[-1])
    for i in range(len(values) - 2, -1, -1):
        out = jnp.where(at == i, jnp.int32(values[i]), out)
    return out


def first_of(bounds, position):
    first = jnp.zeros_like(position)
    for doc in range(1, 4):
        first = jnp.where(bounds[doc] <= position, bounds[doc], first)
    return first


def conv_kernel(group_size, place, bounds, rim_a_ref, rim_b_ref, prod_ref, query_ref, filt_ref, out_ref, mask):
    rows, cols = prod_ref.shape
    step = pl.program_id(0)

    @pl.when(step == 0)
    def _():
        token = place[0] * rows + lax.broadcasted_iota(jnp.int32, (2 * rows, rows), 1)
        source = (place[0] - 1) * rows + lax.broadcasted_iota(jnp.int32, (2 * rows, rows), 0)
        allowed = (source <= token) & (source > token - rows) & (source >= first_of(bounds, token))
        mask[...] = jnp.where(allowed, 1.0, 0.0).astype(jnp.bfloat16)

    rim = jnp.where(step < pl.num_programs(0) // 2, rim_a_ref[...], rim_b_ref[...])
    turned = jnp.concatenate([rim, prod_ref[...]], axis=0).T
    filters = filt_ref[...].astype(jnp.float32)
    allowed = mask[...]
    parts = []
    for g in range(cols // group_size):
        line = jnp.broadcast_to(filters[g : g + 1, :], (rows, rows))
        ring = pltpu.roll(line, 0, 1, stride=1, stride_axis=0).astype(jnp.bfloat16)
        taps = jnp.concatenate([ring, ring], axis=0) * allowed
        parts.append(
            jnp.dot(turned[g * group_size : (g + 1) * group_size], taps, preferred_element_type=jnp.float32)
        )
    total = jnp.concatenate(parts, axis=0).T
    out_ref[...] = (query_ref[...].astype(jnp.float32) * total).astype(out_ref.dtype)


def mixer(place, bounds, rim_a, rim_b, product, mix_query, mr_filter):
    rows, width = product.shape
    groups, filt_len = mr_filter.shape
    group_size = width // groups
    steps = width // COLS
    tile = pl.BlockSpec((rows, COLS), lambda i, *_: (0, i))
    return pl.pallas_call(
        functools.partial(conv_kernel, group_size),
        out_shape=jax.ShapeDtypeStruct((rows, width), jnp.bfloat16),
        grid_spec=pltpu.PrefetchScalarGridSpec(
            num_scalar_prefetch=2,
            grid=(steps,),
            in_specs=[
                pl.BlockSpec((rows, COLS), lambda i, *_: (0, jnp.minimum(i, steps // 2 - 1))),
                pl.BlockSpec((rows, COLS), lambda i, *_: (0, jnp.maximum(i - steps // 2, 0))),
                tile,
                tile,
                pl.BlockSpec((COLS // group_size, filt_len), lambda i, *_: (i, 0)),
            ],
            out_specs=tile,
            scratch_shapes=[pltpu.VMEM((2 * rows, rows), jnp.bfloat16)],
        ),
        cost_estimate=pl.CostEstimate(
            flops=2 * rows * 2 * filt_len * width * 16, bytes_accessed=8 * rows * width, transcendentals=0
        ),
        name="mixer",
    )(place, bounds, rim_a, rim_b, product, mix_query, mr_filter)


def cols_of(h):
    return slice(h * HEAD_DIM, (h + 1) * HEAD_DIM)


def fold_tiles(bounds, query_block, query, sources, heads, state, finish, tile=2 * SUB, turn=None):
    top, den, acc, turned_q, turned_v = state
    rows = query.shape[0]
    turned_q[...] = query.T
    whole_lowest = first_of(bounds, query_block * rows)
    for n, (block, _, value_of) in enumerate(sources):

        inside = (block >= 0) & (block <= query_block) & ((block + 1) * rows > whole_lowest)

        @pl.when(inside if turn is None else turn)
        def _(n=n, value_of=value_of):
            turned_v[n] = value_of().T

    for part in range(rows // SUB):
        at = pl.ds(part * SUB, SUB)
        query_from = query_block * rows + part * SUB
        line_pos = query_from + lax.broadcasted_iota(jnp.int32, (1, SUB), 1)
        first_row = first_of(bounds, line_pos)
        lowest = first_of(bounds, query_from)
        top[...] = jnp.full(top.shape, 0.5 * NEG_FILL, jnp.float32)
        den[...] = jnp.zeros(den.shape, jnp.float32)
        acc[...] = jnp.zeros(acc.shape, jnp.float32)
        for n, (block, key_of, _) in enumerate(sources):
            for piece in range(rows // tile):
                key_from = block * rows + piece * tile
                needed = (block >= 0) & (key_from <= query_from) & (key_from + tile > lowest)

                @pl.when(needed)
                def _(n=n, key_of=key_of, piece=piece, key_from=key_from):
                    take = pl.ds(piece * tile, tile)
                    key_pos = key_from + lax.broadcasted_iota(jnp.int32, (tile, SUB), 0)
                    allowed = (key_pos <= line_pos) & (key_pos >= first_row)
                    scores = [
                        jnp.dot(key_of(h, take), turned_q[cols_of(h), at], preferred_element_type=jnp.float32)
                        for h in range(heads)
                    ]
                    ready = []
                    for h in range(heads):
                        masked = jnp.where(allowed, scores[h], NEG_FILL)
                        old = top[h]
                        new = jnp.maximum(old, jnp.max(masked, axis=0, keepdims=True))
                        weights = jnp.exp2((masked - new) * LOG2_SCALE)
                        factor = jnp.exp2((old - new) * LOG2_SCALE)
                        den[h] = den[h] * factor + jnp.sum(weights, axis=0, keepdims=True)
                        top[h] = new
                        ready.append((weights.astype(jnp.bfloat16), factor))
                    for h, (weights, factor) in enumerate(ready):
                        acc[h] = acc[h] * factor + jnp.dot(
                            turned_v[n, cols_of(h), take], weights, preferred_element_type=jnp.float32
                        )

        for h in range(heads):
            some = den[h] > 0.0
            safe = jnp.where(some, den[h], 1.0)
            lse = jnp.where(some, top[h] * LOG2_SCALE + jnp.log2(safe), NEG_FILL)
            finish(h, at, acc[h] / safe, lse)


def write_message(out_ref, h, at, scaled, lse):
    out_ref[h, :HEAD_DIM, at] = scaled.astype(jnp.bfloat16)
    high = lse.astype(jnp.bfloat16).astype(jnp.float32)
    mid = (lse - high).astype(jnp.bfloat16).astype(jnp.float32)
    low = lse - high - mid
    line = lax.broadcasted_iota(jnp.int32, (EXTRA, SUB), 0)
    lines = jnp.where(line == 0, high, jnp.where(line == 1, mid, low))
    out_ref[h, HEAD_DIM:, at] = lines.astype(jnp.bfloat16)


def write_kept(out_ref, lse_ref, h, at, scaled, lse):
    out_ref[h, :, at] = scaled
    lse_ref[h, :, at] = jnp.broadcast_to(lse, (8, SUB))


def ctx_of(place):
    return place[0] // HEADS_AXIS


def late_side(place):
    return jnp.where(ctx_of(place) < 2, 0, 1)


def early_side(place):
    return jnp.where(ctx_of(place) == 0, 1, 0)


def own_source(block, k_ref, v_ref):
    return block, lambda h, take: k_ref[take, cols_of(h)], lambda: v_ref[...]


def fetch(place, left_ref, right_ref, held, sem):
    left = ctx_of(place) < 2

    @pl.when(left)
    def _():
        copy = pltpu.make_async_copy(left_ref, held, sem)
        copy.start()
        copy.wait()

    @pl.when(jnp.logical_not(left))
    def _():
        copy = pltpu.make_async_copy(right_ref, held, sem)
        copy.start()
        copy.wait()


def got_source(block, held):
    return block, lambda h, take: held[0, take, cols_of(h)], lambda: held[1]


def own_kernel(place, bounds, q_ref, k_ref, v_ref, out_ref, lse_ref, *state):
    ctx = ctx_of(place)
    finish = functools.partial(write_kept, out_ref, lse_ref)
    fold_tiles(bounds, ctx, q_ref[...], [own_source(ctx, k_ref, v_ref)], SIDE, state, finish, SUB)


def early_kernel(place, bounds, q_ref, k_ref, v_ref, out_ref, *state):
    ctx = ctx_of(place)

    @pl.when((ctx == 0) | (ctx == 2))
    def _():
        finish = functools.partial(write_message, out_ref)
        fold_tiles(bounds, ctx + 1, q_ref[...], [own_source(ctx, k_ref, v_ref)], SIDE, state, finish)


def carry_kernel(place, bounds, ql_ref, qr_ref, k_ref, v_ref, out_ref, lse_ref, *state):
    ctx = ctx_of(place)

    @pl.when(ctx < 3)
    def _():
        query = jnp.where(ctx < 2, ql_ref[...], qr_ref[...])
        finish = functools.partial(write_kept, out_ref, lse_ref)
        fold_tiles(
            bounds, pick(ctx, 3, 2, 3, 2), query, [own_source(ctx, k_ref, v_ref)], SIDE, state, finish
        )


def late_kernel(
    place, bounds, ql_ref, qr_ref, part_ref, part_lse, q_ref, left_ref, right_ref, out_ref, got_ref, got_lse,
    held, sem, *state
):
    ctx = ctx_of(place)
    fetch(place, left_ref, right_ref, held, sem)
    query = jnp.where(ctx < 2, ql_ref[...], qr_ref[...])
    carried = ctx < 3
    source = got_source(pick(ctx, 1, 0, 1, 0), held)

    def finish(h, at, scaled, lse):
        other = jnp.where(carried, part_lse[h, 0:1, at], NEG_FILL)
        before = jnp.where(carried, part_ref[h, :, at], 0.0)
        peak = jnp.maximum(lse, other)
        here, there = jnp.exp2(lse - peak), jnp.exp2(other - peak)
        both = here + there
        write_message(out_ref, h, at, (scaled * here + before * there) / both, peak + jnp.log2(both))

    fold_tiles(bounds, pick(ctx, 3, 2, 3, 2), query, [source], SIDE, state, finish, turn=ctx >= 0)

    @pl.when(ctx >= 1)
    def _():
        keep = functools.partial(write_kept, got_ref, got_lse)
        fold_tiles(bounds, ctx, q_ref[...], [source], SIDE, state, keep, turn=ctx < 0)


def fold_call(kernel, name, work, rows, steps, in_specs, message, got, arrays, place, bounds):
    half = SIDE * HEAD_DIM
    out_shape, out_specs = (), ()
    if message:
        out_shape = (jax.ShapeDtypeStruct((steps * SIDE, HEAD_DIM + EXTRA, rows), jnp.bfloat16),)
        out_specs = (pl.BlockSpec((SIDE, HEAD_DIM + EXTRA, rows), lambda i, *_: (i, 0, 0)),)
    if got or not message:
        out_shape += (
            jax.ShapeDtypeStruct((steps * SIDE, HEAD_DIM, rows), jnp.float32),
            jax.ShapeDtypeStruct((steps * SIDE, 8, rows), jnp.float32),
        )
        out_specs += (
            pl.BlockSpec((SIDE, HEAD_DIM, rows), lambda i, *_: (i, 0, 0)),
            pl.BlockSpec((SIDE, 8, rows), lambda i, *_: (i, 0, 0)),
        )
    scratch = [pltpu.VMEM((2, rows, half), jnp.bfloat16), pltpu.SemaphoreType.DMA] if got else []
    scratch += [
        pltpu.VMEM((SIDE, 1, SUB), jnp.float32),
        pltpu.VMEM((SIDE, 1, SUB), jnp.float32),
        pltpu.VMEM((SIDE, HEAD_DIM, SUB), jnp.float32),
        pltpu.VMEM((half, rows), jnp.bfloat16),
        pltpu.VMEM((1, half, rows), jnp.bfloat16),
    ]
    return pl.pallas_call(
        kernel,
        out_shape=out_shape,
        grid_spec=pltpu.PrefetchScalarGridSpec(
            num_scalar_prefetch=2, grid=(steps,), in_specs=in_specs, out_specs=out_specs, scratch_shapes=scratch
        ),
        cost_estimate=pl.CostEstimate(flops=work, bytes_accessed=1, transcendentals=0),
        name=name,
    )(place, bounds, *arrays)


def pack_kernel(place, q_ref, k_ref, v_ref, left, right, q_l, q_r, q_x, held, in_sems, out_sems):
    half = SIDE * HEAD_DIM
    low, high = pl.ds(0, half), pl.ds(half, half)
    reads = [
        pltpu.make_async_copy(ref.at[:, cols], held.at[n], in_sems.at[n])
        for n, (ref, cols) in enumerate(
            [(k_ref, low), (v_ref, low), (k_ref, high), (v_ref, high), (q_ref, low), (q_ref, high)]
        )
    ]
    writes = [
        pltpu.make_async_copy(held.at[0:2], left, out_sems.at[0]),
        pltpu.make_async_copy(held.at[2:4], right, out_sems.at[1]),
        pltpu.make_async_copy(held.at[4], q_l, out_sems.at[2]),
        pltpu.make_async_copy(held.at[5], q_r, out_sems.at[3]),
        pltpu.make_async_copy(held.at[jnp.where(ctx_of(place) == 3, 4, 5)], q_x, out_sems.at[4]),
    ]
    for copy in reads:
        copy.start()
    for n, copy in enumerate(reads):
        copy.wait()
        for ready in {1: [0], 3: [1], 4: [2], 5: [3, 4]}.get(n, []):
            writes[ready].start()
    for copy in writes:
        copy.wait()


def pack(place, queries, keys, values):
    rows = keys.shape[0]
    half = SIDE * HEAD_DIM
    anywhere = pl.BlockSpec(memory_space=pl.ANY)
    both = jax.ShapeDtypeStruct((2, rows, half), jnp.bfloat16)
    single = jax.ShapeDtypeStruct((rows, half), jnp.bfloat16)
    return pl.pallas_call(
        pack_kernel,
        out_shape=(both, both, single, single, single),
        grid_spec=pltpu.PrefetchScalarGridSpec(
            num_scalar_prefetch=1,
            grid=(1,),
            in_specs=[anywhere] * 3,
            out_specs=[anywhere] * 5,
            scratch_shapes=[
                pltpu.VMEM((6, rows, half), jnp.bfloat16),
                pltpu.SemaphoreType.DMA((6,)),
                pltpu.SemaphoreType.DMA((5,)),
            ],
        ),
        name="pack",
    )(place, queries, keys, values)


def merge_kernel(place, own, own_lse, got, got_lse, one_ref, two_ref, three_ref, out_ref):
    ctx = ctx_of(place)

    def sent(ref, flag, h):
        tail = ref[h, HEAD_DIM:, :].astype(jnp.float32)
        lse = jnp.where(flag, tail[0:1, :] + tail[1:2, :] + tail[2:3, :], NEG_FILL)
        return jnp.where(flag, ref[h, :HEAD_DIM, :].astype(jnp.float32), 0.0), lse

    def kept(ref, lse_ref, flag, h):
        return jnp.where(flag, ref[h], 0.0), jnp.where(flag, lse_ref[h, 0:1, :], NEG_FILL)

    def combine(others):
        for h in range(SIDE):
            parts = [(own[h], own_lse[h, 0:1, :])] + others(h)
            peak = functools.reduce(jnp.maximum, [lse for _, lse in parts])
            shares = [jnp.exp2(lse - peak) for _, lse in parts]
            inverse = 1.0 / functools.reduce(jnp.add, shares)
            summed = functools.reduce(jnp.add, [out * (share * inverse) for (out, _), share in zip(parts, shares)])
            out_ref[:, cols_of(h)] = summed.astype(out_ref.dtype).T

    @pl.when(pl.program_id(0) == 0)
    def _():
        combine(
            lambda h: [kept(got, got_lse, ctx == 1, h), sent(one_ref, ctx >= 2, h), sent(three_ref, ctx == 3, h)]
        )

    @pl.when(pl.program_id(0) == 1)
    def _():
        combine(
            lambda h: [kept(got, got_lse, ctx >= 2, h), sent(two_ref, ctx >= 2, h), sent(three_ref, ctx == 1, h)]
        )


def merge(place, own, got, one, two, three):
    rows = one.shape[2]
    tall = HEAD_DIM + EXTRA
    moving = lambda i, *_: (i, 0, 0)
    fixed = lambda i, *_: (0, 0, 0)
    pair = lambda at: [pl.BlockSpec((SIDE, HEAD_DIM, rows), at), pl.BlockSpec((SIDE, 8, rows), at)]
    return pl.pallas_call(
        merge_kernel,
        out_shape=jax.ShapeDtypeStruct((rows, 2 * SIDE * HEAD_DIM), jnp.bfloat16),
        grid_spec=pltpu.PrefetchScalarGridSpec(
            num_scalar_prefetch=1,
            grid=(2,),
            in_specs=pair(moving) + pair(fixed) + [pl.BlockSpec((SIDE, tall, rows), fixed)] * 3,
            out_specs=pl.BlockSpec((rows, SIDE * HEAD_DIM), lambda i, *_: (0, i)),
        ),
        name="merge",
    )(place, *own, *got, one, two, three)


def on_device(mix_query, mix_key, mix_value, mr_filter, doc_ids, att_query, att_key, att_value):
    at_head = lax.axis_index("head")
    heads = lax.axis_size("head")
    blocks = lax.axis_size("ctx")
    half = SIDE * HEAD_DIM
    rows = att_key.shape[0]

    def pass_on(x, *pairs):
        return lax.ppermute(x, "ctx", list(pairs))

    place = jnp.reshape(lax.axis_index(("ctx", "head")), (1,)).astype(jnp.int32)
    pack_l, pack_r, query_l, query_r, query_x = pack(place, att_query, att_key, att_value)
    pack_l, pack_r, query_l, query_r, query_x, doc_ids, att_query, mix_key = lax.optimization_barrier(
        (pack_l, pack_r, query_l, query_r, query_x, doc_ids, att_query, mix_key)
    )
    kv_l = pass_on(pack_l, (0, 1), (1, 0))
    kv_r = pass_on(pack_r, (0, 3), (1, 2))
    q_x = pass_on(query_x, (3, 2), (1, 0))
    q_l = pass_on(query_l, (2, 1), (3, 0))
    q_r = pass_on(query_r, (2, 3), (3, 2))
    bounds = jnp.sum((doc_ids[None, :] < jnp.arange(4, dtype=jnp.int32)[:, None]).astype(jnp.int32), axis=1)

    product = (mix_key.astype(jnp.float32) * mix_value.astype(jnp.float32)).astype(jnp.bfloat16)
    width = product.shape[1]
    count = blocks * heads

    whole = pl.BlockSpec((rows, half), lambda i, *_: (0, 0))
    stepped = pl.BlockSpec((rows, half), lambda i, *_: (0, i))
    at_early = pl.BlockSpec((rows, half), lambda i, place, bounds: (0, early_side(place)))
    at_late = pl.BlockSpec((rows, half), lambda i, place, bounds: (0, late_side(place)))
    anywhere = pl.BlockSpec(memory_space=pl.ANY)
    part = [
        pl.BlockSpec((SIDE, HEAD_DIM, rows), lambda i, *_: (0, 0, 0)),
        pl.BlockSpec((SIDE, 8, rows), lambda i, *_: (0, 0, 0)),
    ]

    own = fold_call(
        own_kernel, "fold_own", 1, rows, 2, [stepped] * 3, False, False,
        (att_query, att_key, att_value), place, bounds,
    )
    own, q_x, q_l, q_r, product = lax.optimization_barrier((own, q_x, q_l, q_r, product))
    (early,) = fold_call(
        early_kernel, "fold_early", 1, rows, 1, [whole, at_early, at_early], True, False,
        (q_x, att_key, att_value), place, bounds,
    )
    part_3 = pass_on(early, (0, 1), (2, 3))
    q_l, q_r, early = lax.optimization_barrier((q_l, q_r, early))
    carry = fold_call(
        carry_kernel, "fold_carry", 1, rows, 1, [whole, whole, at_late, at_late], False, False,
        (q_l, q_r, att_key, att_value), place, bounds,
    )
    carry, kv_l, kv_r, product = lax.optimization_barrier((carry, kv_l, kv_r, product))
    prod_a, prod_b = product[:, : width // 2], product[:, width // 2 :]
    rim_a = lax.ppermute(prod_a, ("ctx", "head"), [(i, i + 1) for i in range(count - 1)])
    staged = lax.ppermute(
        prod_b, ("ctx", "head"), [(i, i + heads) for i in range(count - heads) if i % heads == heads - 1]
    )
    late, *got = fold_call(
        late_kernel, "fold_late", 1, rows, 1, [whole, whole, *part, at_late, anywhere, anywhere], True, True,
        (q_l, q_r, *carry, att_query, kv_l, kv_r), place, bounds,
    )
    part_1 = pass_on(late, (0, 3), (1, 2))
    part_2 = pass_on(late, (2, 3), (3, 2))
    staged, prod_b, late, got = lax.optimization_barrier((staged, prod_b, late, got))
    rim_b = lax.ppermute(
        jnp.where(at_head == heads - 1, staged, prod_b), "head", [(i, (i + 1) % heads) for i in range(heads)]
    )
    mixed = mixer(place, bounds, rim_a, rim_b, product, mix_query, mr_filter)
    place, mixed = lax.optimization_barrier((place, mixed))
    attended = merge(place, own, got, part_1, part_2, part_3)
    return (mixed, attended)


def solution(mesh):
    placed = (
        P(("dp", "ctx", "head"), None),
        P(("dp", "ctx", "head"), None),
        P(("dp", "ctx", "head"), None),
        P(),
        P("dp"),
        P(("dp", "ctx"), "head"),
        P(("dp", "ctx"), "head"),
        P(("dp", "ctx"), "head"),
    )
    return jax.shard_map(
        on_device,
        mesh=mesh,
        in_specs=placed,
        out_specs=(P(("dp", "ctx", "head"), None), P(("dp", "ctx"), "head")),
        check_vma=False,
    )
```
